32 devices in a mesh: row: 8 (over y, x, core), col: 4 (over z).
Axes of the slice: x: 2, y: 2, z: 4, core: 2. Of those that a mesh axis runs over, the one named last changes fastest.
Arguments:
- tile_values: bfloat16 [8, 4, 64, 128, 128], P('row', 'col'), may hold values from -0.0625 to 0.0625
- tile_row: int32 [8, 4, 64], P('row', 'col'), may hold values from 0 to 3
- tile_col: int32 [8, 4, 64], P('row', 'col'), may hold values from 0 to 3
- tile_count: int32 [8, 4], P('row', 'col'), may hold values from 16 to 64, as said below
- primal_init: float32 [64, 2048], P(None, ('row', 'col')), may hold values from -3 to 3
- dual_init: float32 [64, 4096], P(None, ('row', 'col')), may hold values from -3 to 3
- cost_vector: float32 [2048], P(('row', 'col')), may hold values from -4 to 4
- lower_bound: float32 [2048], P(('row', 'col')), may hold values from -1 to -0.2
- upper_bound: float32 [2048], P(('row', 'col')), may hold values from 0.2 to 1
- bound_kind: int32 [2048], P(('row', 'col')), may hold values from 0 to 2
- row_kind: int32 [4096], P(('row', 'col')), may hold values from 0 to 1
- demand: float32 [64, 4096], P(None, ('row', 'col')), may hold values from -20 to 20
Outputs:
- primal_out: float32 [64, 2048], P(None, ('row', 'col'))
- dual_out: float32 [64, 4096], P(None, ('row', 'col'))
- residual_norm: float32 [3, 64], replicated
The draws below stay inside these ranges and needn't reach their ends.
Inputs may be any that keep to these rules, and one draw needn't show every extreme that they name: `tile_count`: live tile slots of one device; some device has all 64 slots live.
All inputs are finite; a program needn't handle non-finite values.
Results may differ from the reference program's by a relative error of at most 0.0022.
Values may be sent and summed in bfloat16 or wider, within the bound.
A program may use at most 64 MiB of HBM per device.

```python
import jax
import jax.numpy as jnp
from jax import lax

TILE = 128
SCEN = 64
TCAP = 64
ITERS = 3
VAR_DEV = 64
NCOL = 2048
NROWS = 4096
N_ROW = 8
N_COL = 4


def draw_tile_count(key, part):
    first_key, second_key = jax.random.split(key)
    total_lists = N_ROW * N_COL
    counts = jax.random.randint(first_key, (total_lists,), max(TCAP // 4, 1), TCAP + 1)
    chosen = jax.random.randint(second_key, (), 0, total_lists)
    counts = jnp.where(jnp.arange(total_lists) == chosen, TCAP, counts)
    return counts.reshape(N_ROW, N_COL).astype(jnp.int32)


def draw_demand(key, part):
    row_place = jnp.arange(NROWS, dtype=jnp.float32) / NROWS
    scen_place = jnp.arange(SCEN, dtype=jnp.float32) / SCEN
    scale = 0.5 * (10.0 ** (0.5 * row_place))[None, :] * (10.0 ** (0.5 * scen_place))[:, None]
    base = jnp.clip(jax.random.normal(key, (SCEN, NROWS), jnp.float32), -4.0, 4.0)
    return (base * scale).astype(jnp.float32)


def touch_ends(result, stream_key, low, top_value):
    place = [jax.random.randint(jax.random.fold_in(stream_key, axis), (), 0, length) for axis, length in enumerate(result.shape)]
    main_axis = result.shape.index(max(result.shape))
    beside = place[:main_axis] + [(place[main_axis] + 1) % result.shape[main_axis]] + place[main_axis + 1:]
    return result.at[tuple(place)].set(low).at[tuple(beside)].set(top_value)


def shard_levels(stream_key, dims, shards, least, largest):
    gain = 1.0
    for position, shards_of in shards:
        steps = jax.random.uniform(jax.random.fold_in(jax.random.fold_in(stream_key, 6), position), (shards_of,), jnp.float32, least / len(shards), largest / len(shards))
        gain = gain * jnp.repeat(jnp.exp(steps), dims[position] // shards_of).reshape((-1,) + (1,) * (len(dims) - 1 - position))
    return gain


def noise(stream_key, shape, deviation, most, cuts=(), kind=jnp.bfloat16):
    values = deviation * jax.random.normal(stream_key, shape, jnp.float32)
    if cuts:
        values = values * shard_levels(stream_key, shape, cuts, -0.22, 0.18)
    return jnp.clip(values, -most, most).astype(kind)


def setup_inputs(seed: int = 0) -> dict:
    splits = jax.random.split(jax.random.key(seed), 13)
    return {
        "tile_values": noise(splits[0], (N_ROW, N_COL, TCAP, TILE, TILE), (TILE * TCAP) ** -0.5, 0.0625, ((0, 8), (1, 4))),
        "tile_row": touch_ends(jax.random.randint(splits[1], (N_ROW, N_COL, TCAP), 0, N_COL), jax.random.fold_in(splits[1], 1), 0, N_COL - 1).astype(jnp.int32),
        "tile_col": touch_ends(jax.random.randint(splits[2], (N_ROW, N_COL, TCAP), 0, N_ROW // 2), jax.random.fold_in(splits[2], 1), 0, (N_ROW // 2) - 1).astype(jnp.int32),
        "tile_count": draw_tile_count(jax.random.fold_in(splits[12], 71), 0),
        "primal_init": noise(splits[4], (SCEN, NCOL), 0.5, 3.0, ((1, 32),), jnp.float32),
        "dual_init": noise(splits[5], (SCEN, NROWS), 0.5, 3.0, ((1, 32),), jnp.float32),
        "cost_vector": noise(splits[6], (NCOL,), 1.0, 4.0, ((0, 32),), jnp.float32),
        "lower_bound": jnp.clip(-1.0 + 0.8 * jax.random.uniform(splits[7], (NCOL,), jnp.float32) ** shard_levels(splits[7], (NCOL,), ((0, 32),), -0.2, 0.2), -1.0, -0.2),
        "upper_bound": jnp.clip(0.2 + 0.8 * jax.random.uniform(splits[8], (NCOL,), jnp.float32) ** shard_levels(splits[8], (NCOL,), ((0, 32),), -0.2, 0.2), 0.2, 1.0),
        "bound_kind": touch_ends(jax.random.randint(splits[9], (NCOL,), 0, 3), jax.random.fold_in(splits[9], 1), 0, 2).astype(jnp.int32),
        "row_kind": touch_ends(jax.random.randint(splits[10], (NROWS,), 0, 2), jax.random.fold_in(splits[10], 1), 0, 1).astype(jnp.int32),
        "demand": draw_demand(jax.random.fold_in(splits[12], 71), 0),
    }


def project_primal(values, lower_bound, upper_bound, bound_kind):
    values = jnp.where((bound_kind <= 1)[None, :], jnp.maximum(values, lower_bound[None, :]), values)
    values = jnp.where((bound_kind == 0)[None, :], jnp.minimum(values, upper_bound[None, :]), values)
    return values

def reference(tile_values, tile_row, tile_col, tile_count, primal_init, dual_init, cost_vector, lower_bound, upper_bound, bound_kind, row_kind, demand):
    devices_all = N_ROW * N_COL
    col_blocks = N_ROW // 2
    flat_tiles = tile_values.reshape(devices_all, TCAP, TILE, TILE)
    flat_rows = tile_row.reshape(devices_all, TCAP)
    flat_cols = tile_col.reshape(devices_all, TCAP)
    flat_count = tile_count.reshape(devices_all)
    device_ids = jnp.arange(devices_all, dtype=jnp.int32)
    slot_ids = jnp.arange(TCAP, dtype=jnp.int32)
    row_ids = jnp.arange(N_COL, dtype=jnp.int32)
    col_ids = jnp.arange(col_blocks, dtype=jnp.int32)

    def apply_forward(extrapolated):
        grouped = extrapolated.reshape(SCEN, col_blocks, 2, N_COL, VAR_DEV)
        grouped = grouped.transpose(3, 1, 0, 2, 4).reshape(N_COL, col_blocks, SCEN, TILE)

        def visit(total, item):
            blocks, rows, cols, count, device = item
            row_index = device // N_COL
            col_index = device % N_COL
            live_mask = (slot_ids < count).astype(jnp.float32)
            picked = grouped[col_index][cols].astype(jnp.float32)
            product = jnp.einsum('tij,tsj->tsi', blocks.astype(jnp.float32), picked, precision=lax.Precision.HIGHEST)
            onehot = (rows[:, None] == row_ids[None, :]).astype(jnp.float32) * live_mask[:, None]
            summed = jnp.einsum('tr,tsi->rsi', onehot, product, precision=lax.Precision.HIGHEST)
            return (total.at[row_index].add(summed), None)
        start = jnp.zeros((N_ROW, N_COL, SCEN, TILE), jnp.float32)
        total, _ = lax.scan(visit, start, (flat_tiles, flat_rows, flat_cols, flat_count, device_ids))
        return total.transpose(2, 0, 1, 3).reshape(SCEN, NROWS)

    def apply_backward(dual_half):
        grouped = dual_half.reshape(SCEN, N_ROW, N_COL, TILE).transpose(1, 2, 0, 3)

        def visit(total, item):
            blocks, rows, cols, count, device = item
            row_index = device // N_COL
            col_index = device % N_COL
            live_mask = (slot_ids < count).astype(jnp.float32)
            picked = grouped[row_index][rows].astype(jnp.float32)
            product = jnp.einsum('tij,tsi->tsj', blocks.astype(jnp.float32), picked, precision=lax.Precision.HIGHEST)
            onehot = (cols[:, None] == col_ids[None, :]).astype(jnp.float32) * live_mask[:, None]
            summed = jnp.einsum('tc,tsj->csj', onehot, product, precision=lax.Precision.HIGHEST)
            return (total.at[col_index].add(summed), None)
        start = jnp.zeros((N_COL, col_blocks, SCEN, TILE), jnp.float32)
        total, _ = lax.scan(visit, start, (flat_tiles, flat_rows, flat_cols, flat_count, device_ids))
        total = total.reshape(N_COL, col_blocks, SCEN, 2, VAR_DEV)
        return total.transpose(2, 1, 3, 0, 4).reshape(SCEN, NCOL)
    primal = primal_init
    dual = dual_init
    norms = []
    for iteration in range(ITERS):
        dual_half = dual.astype(jnp.bfloat16)
        transposed = apply_backward(dual_half)
        primal_next = primal - 0.4 * (cost_vector[None, :] - transposed)
        primal_next = project_primal(primal_next, lower_bound, upper_bound, bound_kind)
        extrapolated = (2.0 * primal_next - primal).astype(jnp.bfloat16)
        image = apply_forward(extrapolated)
        gap_rows = demand - image
        dual = dual + 0.4 * gap_rows
        dual = jnp.where((row_kind == 1)[None, :], jnp.maximum(dual, 0.0), dual)
        primal = primal_next
        norms.append(jnp.sqrt(lax.optimization_barrier(jnp.sum(gap_rows * gap_rows, axis=1)) / NROWS + 1e-06))
    return (primal, dual, jnp.stack(norms))
```

```python
import functools
import math

import jax
import jax.numpy as jnp
from jax import lax
from jax.experimental import pallas as pl
from jax.experimental.pallas import tpu as pltpu
from jax.sharding import PartitionSpec as P

ITERS = 3
PRIMAL_STEP = 0.4
DUAL_STEP = 0.4
NORM_EPS = 1e-06
MESH = pl.DeviceIdType.MESH
CHUNK = 1024
GROUPS = 2
STRIP = 16
VMEM_LARGE = 59 * 1024 * 1024
VMEM_SMALL = 59 * 1024 * 1024
SMALL = 1024 * 1024
DIMS = (((1,), (1,)), ((), ()))


def dot(left, right):
    return jnp.dot(left, right, preferred_element_type=jnp.float32)


def dot_turned(left, right):
    return lax.dot_general(left, right, DIMS, preferred_element_type=jnp.float32)


def aligned(start, unit):
    return start if isinstance(start, int) else pl.multiple_of(start, unit)


def split(whole):
    hi = whole.astype(jnp.bfloat16)
    return hi, (whole - hi.astype(jnp.float32)).astype(jnp.bfloat16)


def step_kernel(
    n_row,
    n_col,
    small,
    rows_ref,
    cols_ref,
    count_ref,
    tiles_ref,
    primal_ref,
    dual_ref,
    cost_ref,
    lower_ref,
    upper_ref,
    bound_ref,
    kind_ref,
    demand_ref,
    primal_out,
    dual_out,
    norm_out,
    tiles,
    full_hi,
    full_lo,
    turned_hi,
    turned_lo,
    var_send,
    var_recv,
    hi_send,
    lo_send,
    lo_recv,
    demand_recv,
    dual_half,
    dual_state,
    point,
    back_recv,
    fwd_recv,
    squares,
    held,
    fin_send,
    fin_recv,
    fin_dual,
    norm_row,
    tile_sem,
    local_sem,
    send_sem,
    recv_sem,
):
    me_r = lax.axis_index("row")
    me_c = lax.axis_index("col")
    chips = n_row // 2
    chip = me_r // 2
    half = lax.rem(me_r, 2)
    parity = lax.rem(me_c, 2)
    pair_c = me_c + 1 - 2 * parity
    scen, tile = dual_ref.shape
    part = scen // 2
    group = part // GROUPS
    width = primal_ref.shape[1]
    rows, cols = n_col * tile, chips * tile
    mid = rows // 2
    sibling = me_r + 1 - 2 * half
    slots = tiles.shape[0]

    def row_peer(k):
        return lax.rem(me_r + k, n_row)

    def col_peer(k):
        return lax.rem(me_c + k, n_col)

    def greet(r, c):
        pl.semaphore_signal(
            barrier, inc=1, device_id={"row": r, "col": c}, device_id_type=MESH
        )

    barrier = pltpu.get_barrier_semaphore()
    for k in range(1, n_col):
        for r in (me_r, sibling):
            greet(r, col_peer(k))
    for k in range(1, n_row):
        greet(row_peer(k), me_c)
    for k in range(1, chips):
        for h in range(2):
            greet(2 * lax.rem(chip + k, chips) + h, pair_c)

    strips = tile // STRIP
    loads = []
    for q in range(0, strips, 2):
        where = pl.ds(q * STRIP, 2 * STRIP)
        load = pltpu.make_async_copy(
            tiles_ref.at[0, 0, :, where, :], tiles.at[:, where, :], tile_sem.at[q // 2]
        )
        load.start()
        loads.append(load)

    def place(block, other=0):
        start = lax.rem(block, 2) * rows + other * mid + (block // 2) * tile
        return pl.ds(pl.multiple_of(start, tile), tile)

    def scens(index):
        return pl.ds(pl.multiple_of(index * part, part), part)

    started = []
    next_sem = [0]

    def send(src, dst, r, c):
        sem = next_sem[0]
        next_sem[0] += 1
        copy = pltpu.make_async_remote_copy(
            src_ref=src,
            dst_ref=dst,
            send_sem=send_sem.at[sem],
            recv_sem=recv_sem.at[sem],
            device_id={"row": r, "col": c},
            device_id_type=MESH,
        )
        copy.start()
        return copy

    def finish(copies):
        for copy in copies:
            copy.wait_recv()
        started.extend(copies)

    for h in range(2):
        span = slice(h * part, (h + 1) * part)
        hi, lo = split(dual_ref[span, :])
        hi_send[span, :] = hi
        lo_send[h, 0:part] = lo
        kinds = jnp.broadcast_to(kind_ref[...].reshape(1, tile), (16, tile))
        lo_send[h, part : part + 16] = kinds.astype(jnp.float32).astype(jnp.bfloat16)
    kind = bound_ref[...].reshape(1, width)
    bounds = (
        cost_ref[...].reshape(1, width),
        jnp.where(kind <= 1, lower_ref[...].reshape(1, width), -jnp.inf),
        jnp.where(kind == 0, upper_ref[...].reshape(1, width), jnp.inf),
    )
    var_send[...] = jnp.zeros_like(var_send)
    for h in range(2):
        var_send[h, 0:part, 0:width] = primal_ref[h * part : (h + 1) * part, :]
        for index, value in enumerate(bounds):
            var_send[h, part + index : part + index + 1, 0:width] = value
    var_recv[me_r] = var_send[half]
    norm_row[parity * n_row + me_r] = jnp.zeros(norm_row.shape[1:], jnp.float32)
    own = [
        pltpu.make_async_copy(hi_send.at[scens(half)], dual_half.at[:, place(me_c)], local_sem.at[0]),
        pltpu.make_async_copy(lo_send.at[half], lo_recv.at[:, place(me_c)], local_sem.at[1]),
        pltpu.make_async_copy(
            demand_ref.at[scens(half)], demand_recv.at[:, place(me_c)], local_sem.at[2]
        ),
    ]
    for copy in own:
        copy.start()

    pl.semaphore_wait(barrier, (n_row - 1) + 2 * (n_col - 1) + 2 * (chips - 1))

    def spread(mine, other, target):
        copies = []
        for k in range(1, n_col):
            copies.append(send(mine, target.at[:, place(me_c)], me_r, col_peer(k)))
            copies.append(send(other, target.at[:, place(me_c, 1)], sibling, col_peer(k)))
        copies.append(send(other, target.at[:, place(me_c, 1)], sibling, me_c))
        return copies

    first_dual = spread(hi_send.at[scens(half)], hi_send.at[scens(1 - half)], dual_half)
    first_var = []
    for k in range(1, n_row):
        peer = row_peer(k)
        first_var.append(send(var_send.at[lax.rem(peer, 2)], var_recv.at[me_r], peer, me_c))
    first_rest = spread(lo_send.at[half], lo_send.at[1 - half], lo_recv)
    first_rest += spread(demand_ref.at[scens(half)], demand_ref.at[scens(1 - half)], demand_recv)

    deep = slots * STRIP
    slot_of = lax.broadcasted_iota(jnp.int32, (slots, deep), 1) // STRIP
    expand = (slot_of == lax.broadcasted_iota(jnp.int32, (slots, deep), 0)).astype(jnp.float32)
    keys = rows_ref[0].astype(jnp.float32) * chips + cols_ref[0].astype(jnp.float32)
    keys = jnp.broadcast_to(keys, (8, slots)).astype(jnp.bfloat16)
    lane = lax.broadcasted_iota(jnp.int32, (8, deep), 1)
    code = dot(keys, expand.astype(jnp.bfloat16)) * STRIP + (lane % STRIP).astype(jnp.float32)
    live = (lane // STRIP).astype(jnp.float32) < count_ref[...].astype(jnp.float32)
    code = jnp.where(live, code, -1.0)[0:1]
    for load in loads:
        load.wait()
    high = chips * STRIP

    def choose(first):
        row = lax.broadcasted_iota(jnp.int32, (high, deep), 0) + first * high
        return (code == row.astype(jnp.float32)).astype(jnp.float32).astype(jnp.bfloat16)

    def build(blocks):
        chosen = jnp.concatenate([choose(block) for block in blocks], axis=0)
        for q in range(0, strips, 2):
            strip = jnp.concatenate(
                [
                    tiles[:, (q + j) * STRIP : (q + j + 1) * STRIP, :].reshape(deep, tile)
                    for j in range(2)
                ],
                axis=1,
            )
            total = dot(chosen, strip)
            hi, lo = split(total)
            for number, block in enumerate(blocks):
                base = (block % 2) * rows + (block // 2) * tile
                for j in range(2):
                    to = pl.ds(aligned(base + (q + j) * STRIP, STRIP), STRIP)
                    for c in range(chips):
                        at = number * high + c * STRIP
                        part_hi = hi[at : at + STRIP, j * tile : (j + 1) * tile]
                        part_lo = lo[at : at + STRIP, j * tile : (j + 1) * tile]
                        full_hi[to, c * tile : (c + 1) * tile] = part_hi
                        full_lo[to, c * tile : (c + 1) * tile] = part_lo

    blocks = []
    for p in range(2):
        if small:
            build(list(range(p, n_col, 2)))
        else:

            def one(index, carry):
                build([2 * index + p])
                return carry

            lax.fori_loop(0, n_col // 2, one, 0)
        mine, theirs = pl.ds(p * rows, mid), pl.ds(p * rows + mid, mid)
        for matrix in (full_hi, full_lo):
            blocks.append(send(matrix.at[mine], matrix.at[theirs], sibling, me_c))

    def multiply(left, matrices, out, flip):
        deep, wide = left.shape[1], out.shape[1]
        step, span = math.gcd(deep, CHUNK), math.gcd(wide, CHUNK)

        def term(d, w):
            x = left[:, d]
            if flip:
                return sum(dot_turned(x, matrix[w, d]) for matrix in matrices)
            return sum(dot(x, matrix[d, w]) for matrix in matrices)

        if step == deep and span == wide:
            out[...] = term(slice(None), slice(None)).astype(out.dtype)
            return

        def column(j, carry):
            w = pl.ds(pl.multiple_of(j * span, span), span)

            def add(i, total):
                return total + term(pl.ds(pl.multiple_of(i * step, step), step), w)

            total = lax.fori_loop(0, deep // step, add, jnp.zeros((left.shape[0], span), jnp.float32))
            out[:, w] = total.astype(out.dtype)
            return carry

        lax.fori_loop(0, wide // span, column, 0)

    def half_rows(which):
        return pl.ds(pl.multiple_of(which * rows, rows), rows)

    spans = [slice(g * group, (g + 1) * group) for g in range(GROUPS)]
    own_half = half_rows(parity)
    everything = pl.ds(0, 2 * rows)

    def settle(it, g):
        span = spans[g]
        lanes = everything if it + 1 < ITERS else own_half
        floor = jnp.where(lo_recv[part : part + 16, lanes][0:1].astype(jnp.float32) == 1.0, 0.0, -jnp.inf)
        if it == 0:
            dual = dual_half[span, lanes].astype(jnp.float32) + lo_recv[span, lanes].astype(jnp.float32)
        else:
            dual = dual_state[span, lanes]
        image = fwd_recv[it, 0, span, lanes].astype(jnp.float32)
        for k in range(1, n_col):
            image = image + fwd_recv[it, k, span, lanes].astype(jnp.float32)
        gap = demand_recv[span, lanes] - image
        dual = jnp.maximum(dual + DUAL_STEP * gap, floor)
        dual_state[span, lanes] = dual
        if it + 1 < ITERS:
            dual_half[span] = dual.astype(jnp.bfloat16)
            gap = jnp.where(parity == 0, gap[:, 0:rows], gap[:, rows:])
        total = gap[:, 0:tile] * gap[:, 0:tile]
        for start in range(tile, rows, tile):
            piece = gap[:, start : start + tile]
            total = total + piece * piece
        squares[span] = total

    def square(it):
        ones = jnp.ones((8, tile), jnp.bfloat16)
        total = sum(dot_turned(ones, term) for term in split(squares[...]))
        norm_row[parity * n_row + me_r, it : it + 1, 0:part] = total[0:1]

    primal_parts = [None] * GROUPS
    for copy in own:
        copy.wait()
    finish(first_dual)
    finish(blocks)
    matrices = (full_hi, full_lo)
    for it in range(ITERS):
        flights = []
        for g, span in enumerate(spans):
            if it > 0:
                finish(arriving[g])
                settle(it - 1, g)
            mine = back_recv.at[it, chip, span]
            multiply(dual_half.at[span], matrices, mine, False)
            flights.append([send(mine, mine, row_peer(2 * k), me_c) for k in range(1, chips)])
        if it == 0:
            finish(first_var)
            state = jnp.concatenate([var_recv[r, :, 0:width] for r in range(n_row)], axis=1)
            primal_parts = [state[span] for span in spans]
            cost, lower, upper = (state[part + i : part + i + 1] for i in range(3))
            if small:
                turned_hi[...] = full_hi[...].T
                turned_lo[...] = full_lo[...].T
        else:
            square(it - 1)
        arriving = []
        for g, span in enumerate(spans):
            finish(flights[g])
            transposed = back_recv[it, 0, span].astype(jnp.float32)
            for k in range(1, chips):
                transposed = transposed + back_recv[it, k, span].astype(jnp.float32)
            primal = primal_parts[g]
            moved = primal - PRIMAL_STEP * (cost - transposed)
            moved = jnp.minimum(jnp.maximum(moved, lower), upper)
            point[span] = (2.0 * moved - primal).astype(jnp.bfloat16)
            primal_parts[g] = moved
            mine = fwd_recv.at[it, me_c, span]
            if small:
                multiply(point.at[span], (turned_hi, turned_lo), mine, False)
            else:
                multiply(point.at[span], matrices, mine, True)
            copies = []
            for k in range(1, n_col):
                peer = col_peer(k)
                lanes = everything if it + 1 < ITERS else half_rows(lax.rem(peer, 2))
                mine = fwd_recv.at[it, me_c, span, lanes]
                copies.append(send(mine, mine, me_r, peer))
            arriving.append(copies)
        if it == 0:
            finish(first_rest)
    first = half == 0
    for g, span in enumerate(spans):
        held[span] = primal_parts[g]
    both = held[:, pl.ds(pl.multiple_of(chip * tile, tile), tile)]
    low, high = both[:, 0:width], both[:, width:]
    fin_send[:, 0:width] = jnp.where(first, high, low)
    fin_send[:, width:] = jnp.zeros((part, tile - width), jnp.float32)
    last_primal = send(fin_send, fin_recv, sibling, me_c)
    primal_out[scens(half), :] = jnp.where(first, low, high)
    for g in range(GROUPS):
        finish(arriving[g])
        settle(ITERS - 1, g)
    square(ITERS - 1)
    mine = norm_row.at[parity * n_row + me_r]
    norms = [send(mine, mine, row_peer(k), me_c) for k in range(1, n_row)]
    norms += [send(mine, mine, row_peer(k), pair_c) for k in range(n_row)]
    last_dual = send(dual_state.at[:, place(me_c, 1)], fin_dual, sibling, me_c)
    dual_out[scens(half), :] = dual_state[:, place(me_c)]
    finish([last_primal])
    primal_out[scens(1 - half), :] = fin_recv[:, 0:width]
    finish([last_dual])
    dual_out[scens(1 - half), :] = fin_dual[...]
    finish(norms)
    for h in range(2):
        total = norm_row[h]
        for r in range(h + 2, 2 * n_row, 2):
            total = total + norm_row[r]
        norm_out[:, h * part : (h + 1) * part] = jnp.sqrt(
            total[0:ITERS, 0:part] / (n_row * n_col * tile) + NORM_EPS
        )
    for copy in started:
        copy.wait_send()


def tail_kernel(primal_ref, dual_ref, norm_ref, primal_out, dual_out, norm_out):
    primal_out[...] = primal_ref[...]
    dual_out[...] = dual_ref[...]
    norm_out[...] = norm_ref[...]


def shards(*arguments):
    tile_values, tile_row, tile_col, tile_count, primal_init, dual_init = arguments[:6]
    n_row = lax.axis_size("row")
    n_col = lax.axis_size("col")
    slots, tile = tile_values.shape[2], tile_values.shape[-1]
    scen, width = primal_init.shape
    part = scen // 2
    chips = n_row // 2
    rows, cols = n_col * tile, chips * tile
    small = rows * cols <= SMALL
    vmem = pl.BlockSpec(memory_space=pltpu.VMEM)
    hbm = pl.BlockSpec(memory_space=pl.ANY)
    sems = ITERS * GROUPS * (chips + n_col) + 3 * (n_row + 2 * n_col) + 8
    f32, bf16 = jnp.float32, jnp.bfloat16
    outs = (
        jax.ShapeDtypeStruct((scen, width), f32),
        jax.ShapeDtypeStruct((scen, tile), f32),
        jax.ShapeDtypeStruct((ITERS, scen), f32),
    )
    turned = (cols, 2 * rows) if small else (16, tile)
    results = pl.pallas_call(
        functools.partial(step_kernel, n_row, n_col, small),
        out_shape=outs,
        in_specs=[vmem] * 3 + [hbm] + [vmem] * 8,
        out_specs=(vmem, vmem, vmem),
        scratch_shapes=[
            pltpu.VMEM((slots, tile, tile), bf16),
            pltpu.VMEM((2 * rows, cols), bf16),
            pltpu.VMEM((2 * rows, cols), bf16),
            pltpu.VMEM(turned, bf16),
            pltpu.VMEM(turned, bf16),
            pltpu.VMEM((2, part + 8, tile), f32),
            pltpu.VMEM((n_row, part + 8, tile), f32),
            pltpu.VMEM((scen, tile), bf16),
            pltpu.VMEM((2, part + 16, tile), bf16),
            pltpu.VMEM((part + 16, 2 * rows), bf16),
            pltpu.VMEM((part, 2 * rows), f32),
            pltpu.VMEM((part, 2 * rows), bf16),
            pltpu.VMEM((part, 2 * rows), f32),
            pltpu.VMEM((part, cols), bf16),
            pltpu.VMEM((ITERS, chips, part, cols), bf16),
            pltpu.VMEM((ITERS, n_col, part, 2 * rows), bf16),
            pltpu.VMEM((part, tile), f32),
            pltpu.VMEM((part, cols), f32),
            pltpu.VMEM((part, tile), f32),
            pltpu.VMEM((part, tile), f32),
            pltpu.VMEM((part, tile), f32),
            pltpu.VMEM((2 * n_row, 8, tile), f32),
            pltpu.SemaphoreType.DMA((tile // (2 * STRIP),)),
            pltpu.SemaphoreType.DMA((3,)),
            pltpu.SemaphoreType.DMA((sems,)),
            pltpu.SemaphoreType.DMA((sems,)),
        ],
        compiler_params=pltpu.CompilerParams(
            collective_id=0,
            has_side_effects=True,
            vmem_limit_bytes=VMEM_SMALL if small else VMEM_LARGE,
        ),
    )(tile_row, tile_col, tile_count, tile_values, *arguments[4:])
    return pl.pallas_call(
        tail_kernel, out_shape=outs, in_specs=[vmem] * 3, out_specs=(vmem, vmem, vmem)
    )(*results)


def solution(mesh):
    return jax.shard_map(
        shards,
        mesh=mesh,
        in_specs=(
            P("row", "col", None, None, None),
            P("row", "col", None),
            P("row", "col", None),
            P("row", "col"),
            P(None, ("row", "col")),
            P(None, ("row", "col")),
            P(("row", "col")),
            P(("row", "col")),
            P(("row", "col")),
            P(("row", "col")),
            P(("row", "col")),
            P(None, ("row", "col")),
        ),
        out_specs=(P(None, ("row", "col")), P(None, ("row", "col")), P()),
        check_vma=False,
    )
```
